32 devices in a mesh: seg: 4 (over z), blk: 8 (over y, x, core).
Axes of the slice: x: 2, y: 2, z: 4, core: 2. Of those that a mesh axis runs over, the one named last changes fastest.
Arguments:
- train_acts: bfloat16 [4, 1024, 512], P('seg', 'blk'), may hold values from -6 to 6
- train_grads: bfloat16 [4, 1024, 4096], P('seg', 'blk'), may hold values from -0.0059814453 to 0.0059814453
- counts: int32 [8], replicated, may hold values from 1 to 2, as said below
- basis_in: bfloat16 [4, 1, 512, 512], P('seg'), may hold values from -1 to 1, as said below
- basis_out: bfloat16 [4, 8, 512, 512], P('seg', 'blk'), may hold values from -1 to 1, as said below
- eigenvalues: bfloat16 [4, 8, 512, 512], P('seg', 'blk'), may hold values from 0.049804688 to 5
- back_weight: bfloat16 [4, 8, 512, 512], P('seg', 'blk'), may hold values from -0.25 to 0.25
- derivative: bfloat16 [4, 4, 32, 4096], P('seg', None, None, 'blk'), may hold values from 0 to 1
- query_acts: bfloat16 [4, 4, 32, 512], P('seg'), may hold values from -6 to 6
- query_top: bfloat16 [4, 32, 4096], P(None, None, 'blk'), may hold values from -0.0059814453 to 0.0059814453
Outputs:
- scores: float32 [4, 16], P(None, 'blk')
The draws below stay inside these ranges and needn't reach their ends.
Inputs may be any that keep to these rules, and one draw needn't show every extreme that they name: In each pair of indices 2k and 2k+1 of blk one count is 2 and the other 1, so all counts add up to 12; slots below a device's count are valid. `basis_in`: each 512 x 512 matrix is orthogonal up to rounding. `basis_out`: each 512 x 512 matrix is orthogonal up to rounding.
All inputs are finite; a program needn't handle non-finite values.
Results may differ from the reference program's by a relative error of at most 0.015.
Values may be sent and summed in bfloat16 or wider, within the bound.
A program may use at most 64 MiB of HBM per device.

```python
import math
import jax
import jax.numpy as jnp
from jax import lax

D_BLK = 512
IN_SL = 1
QUERIES = 4
QT = 32
TB = 64
SLOTS = 2
SEGS = 4
OUT_SL = 8
IN = 512
OUT = 4096
TOKENS = 1024


def draw_counts(key, part):
    which = jax.random.randint(jax.random.fold_in(key, 37), (OUT_SL // 2,), 0, 2).astype(jnp.int32)
    paired = jnp.stack([1 + which, 2 - which], axis=1)
    return paired.reshape(OUT_SL).astype(jnp.int32)


def draw_basis_in(key, part):
    raw = jax.random.normal(jax.random.fold_in(key, 11), (SEGS, IN_SL, D_BLK, D_BLK), jnp.float32)
    ortho, upper = jnp.linalg.qr(raw)
    return ortho.astype(jnp.bfloat16)


def draw_basis_out(key, part):
    raw = jax.random.normal(jax.random.fold_in(key, 23), (SEGS, OUT_SL, D_BLK, D_BLK), jnp.float32)
    ortho, upper = jnp.linalg.qr(raw)
    return ortho.astype(jnp.bfloat16)


def level_of(own_key, dims, pieces, least, largest):
    level = 1.0
    for position, blocks in pieces:
        heights = jax.random.uniform(jax.random.fold_in(jax.random.fold_in(own_key, 6), position), (blocks,), jnp.float32, least / len(pieces), largest / len(pieces))
        level = level * jnp.repeat(jnp.exp(heights), dims[position] // blocks).reshape((-1,) + (1,) * (len(dims) - 1 - position))
    return level


def normal_values(rng, shape, scale, bound, split=(), held_as=jnp.bfloat16):
    gain = level_of(rng, shape, split, -0.22, 0.18) if split else 1.0
    drawn = jax.random.normal(rng, shape, jnp.float32) * scale * gain
    return jnp.minimum(jnp.maximum(drawn, -bound), bound).astype(held_as)


def setup_inputs(seed: int = 0) -> dict:
    seeds = jax.random.split(jax.random.key(seed), 11)
    train_acts = normal_values(seeds[0], (SEGS, TOKENS, IN), 1.0, 6.0, ((0, 4), (1, 8)))
    train_grads = normal_values(seeds[1], (SEGS, TOKENS, OUT), 0.001, 0.0059814453, ((0, 4), (1, 8)))
    counts = draw_counts(jax.random.fold_in(seeds[10], 71), 0)
    basis_in = draw_basis_in(jax.random.fold_in(seeds[10], 71), 0)
    basis_out = draw_basis_out(jax.random.fold_in(seeds[10], 71), 0)
    eigenvalues = jnp.clip(jnp.exp(math.log(5.0) - 4.609084 * jax.random.uniform(seeds[5], (SEGS, OUT_SL, D_BLK, IN), jnp.float32) ** level_of(seeds[5], (SEGS, OUT_SL, D_BLK, IN), ((0, 4), (1, 8)), -0.2, 0.2)), 0.049804688, 5.0).astype(jnp.bfloat16)
    back_weight = normal_values(seeds[6], (SEGS, OUT_SL, D_BLK, D_BLK), D_BLK ** -0.5, 0.25, ((0, 4), (1, 8)))
    derivative = jnp.clip(1.0 * jax.random.uniform(seeds[7], (SEGS, QUERIES, QT, OUT), jnp.float32) ** level_of(seeds[7], (SEGS, QUERIES, QT, OUT), ((0, 4), (3, 8)), -0.2, 0.2), 0.0, 1.0).astype(jnp.bfloat16)
    query_acts = normal_values(seeds[8], (SEGS, QUERIES, QT, IN), 1.0, 6.0, ((0, 4),))
    query_top = normal_values(seeds[9], (QUERIES, QT, OUT), 0.001, 0.0059814453, ((2, 8),))
    return dict(train_acts=train_acts, train_grads=train_grads, counts=counts, basis_in=basis_in, basis_out=basis_out, eigenvalues=eigenvalues, back_weight=back_weight, derivative=derivative, query_acts=query_acts, query_top=query_top)


damping = 0.05

def reference(train_acts, train_grads, counts, basis_in, basis_out, eigenvalues, back_weight, derivative, query_acts, query_top):
    f32 = jnp.float32
    b16 = jnp.bfloat16
    seg_count = train_acts.shape[0]
    queries, query_tok, out_width = query_top.shape
    blk_width = basis_out.shape[-1]
    out_slices = basis_out.shape[1]
    in_slices = basis_in.shape[1]
    in_width = in_slices * blk_width
    n_slot = train_acts.shape[1] // TB
    current = query_top
    errors = [current]
    for segment in range(seg_count - 1, 0, -1):
        shaped = current.reshape(queries, query_tok, out_slices, blk_width).astype(f32)
        mixed = jnp.einsum('qtod,ode->qtoe', shaped, back_weight[segment].astype(f32))
        mixed = mixed.reshape(queries, query_tok, out_width)
        current = (current.astype(f32) + mixed * derivative[segment].astype(f32)).astype(b16)
        errors.insert(0, current)
    errors = jnp.stack(errors)

    def per_segment(operands):
        error_seg, acts_seg, inner_basis, outer_basis, eigen_seg, grads_train, acts_train = operands
        err_split = error_seg.reshape(queries, query_tok, out_slices, blk_width).astype(f32)
        rot_err = jnp.einsum('qtod,ode->qtoe', err_split, outer_basis.astype(f32)).astype(b16)
        act_split = acts_seg.reshape(queries, query_tok, in_slices, blk_width).astype(f32)
        rot_acts = jnp.einsum('qtid,ide->qtie', act_split, inner_basis.astype(f32)).astype(b16)
        core_raw = jnp.einsum('qtod,qtie->qodie', rot_err.astype(f32), rot_acts.astype(f32))
        core_raw = core_raw.reshape(queries, out_slices, blk_width, in_width)
        scaled_core = (core_raw / (eigen_seg.astype(f32)[None] + damping)).astype(b16)
        left_prod = jnp.einsum('ocd,qodf->qocf', outer_basis.astype(f32), scaled_core.astype(f32)).astype(b16)
        left_split = left_prod.reshape(queries, out_slices, blk_width, in_slices, blk_width)
        precond = jnp.einsum('qocie,ife->qocif', left_split.astype(f32), inner_basis.astype(f32))
        precond = precond.reshape(queries, out_slices, blk_width, in_width).astype(b16)
        act_slots = acts_train.reshape(n_slot, TB, in_width).astype(f32)
        grad_split = jnp.moveaxis(grads_train.reshape(n_slot * TB, out_slices, blk_width), 1, 0)
        precond_split = jnp.moveaxis(precond, 1, 0)

        def per_slice(slice_ops):
            grads_slice, precond_slice = slice_ops
            grad_slots = grads_slice.reshape(n_slot, TB, blk_width).astype(f32)
            outer_prod = jnp.einsum('ntd,nte->nde', grad_slots, act_slots).astype(b16)
            return jnp.einsum('nde,qde->qn', outer_prod.astype(f32), precond_slice.astype(f32))
        return jnp.sum(lax.map(per_slice, (grad_split, precond_split)), axis=0)
    seg_scores = lax.map(per_segment, (errors, query_acts, basis_in, basis_out, eigenvalues, train_grads, train_acts))
    summed = jnp.sum(seg_scores, axis=0)
    slot_ids = jnp.arange(n_slot, dtype=jnp.int32)
    valid = slot_ids % SLOTS < jnp.take(counts, slot_ids // SLOTS)
    return summed * valid.astype(f32)[None, :]
```

```python
import functools

import jax
import jax.numpy as jnp
from jax import lax
from jax.experimental import pallas as pl
from jax.experimental.pallas import tpu as pltpu
from jax.sharding import PartitionSpec as P

SLOTS = 2
damping = 0.05
F32 = jnp.float32
B16 = jnp.bfloat16
MESH = pl.DeviceIdType.MESH


def kernel(
    segs,
    blks,
    queries,
    counts,
    acts_h,
    grads_h,
    bin_h,
    bout_h,
    eig_h,
    back_h,
    deriv_h,
    qacts_h,
    qtop_h,
    out,
    acts,
    own_g,
    other_g,
    other_a,
    b_in,
    b_out,
    eig,
    back,
    deriv,
    qacts,
    errs,
    moved,
    inv,
    rot_q,
    core_all,
    grads,
    racts,
    part,
    part_in,
    zsum,
    load_sem,
    sel_send,
    sel_recv,
    g0_send,
    g0_recv,
    g1_send,
    g1_recv,
    a_send,
    a_recv,
    f_send,
    e_send,
    e_recv,
    p_send,
    p_recv,
    z_send,
    z_recv,
):
    seg = lax.axis_index("seg")
    blk = lax.axis_index("blk")
    chips = blks // 2
    chip = blk // 2
    lane = blk % 2
    mate_lane = 1 - lane
    mate = chip * 2 + mate_lane
    rows = acts_h.shape[0]
    tb = rows // SLOTS
    half = tb // 2
    per = tb + half
    width = bin_h.shape[0]
    qt = qtop_h.shape[0] // queries

    def remote(src, dst, ssem, rsem, seg_to, blk_to):
        return pltpu.make_async_remote_copy(
            src_ref=src,
            dst_ref=dst,
            send_sem=ssem,
            recv_sem=rsem,
            device_id=(seg_to, blk_to),
            device_id_type=MESH,
        )

    def cols(index):
        return pl.ds(pl.multiple_of(index * width, width), width)

    barrier = pltpu.get_barrier_semaphore()
    for off in range(1, blks):
        pl.semaphore_signal(
            barrier, inc=1, device_id=(seg, lax.rem(blk + off, blks)), device_id_type=MESH
        )
    for off in range(1, segs):
        pl.semaphore_signal(
            barrier, inc=1, device_id=(lax.rem(seg + off, segs), blk), device_id_type=MESH
        )

    keep = pl.ds(pl.multiple_of(tb + lane * half, half), half)
    give = pl.ds(pl.multiple_of(tb + mate_lane * half, half), half)
    mine0 = pl.ds(pl.multiple_of(lane * per, half), tb)
    mine1 = pl.ds(pl.multiple_of(lane * per + tb, half), half)
    mine = pl.ds(pl.multiple_of(lane * per, half), per)
    theirs = pl.ds(pl.multiple_of(mate_lane * per, half), per)

    loads = [
        pltpu.make_async_copy(src, dst, load_sem.at[n])
        for n, (src, dst) in enumerate(
            (
                (back_h, back),
                (deriv_h, deriv),
                (acts_h, acts),
                (bin_h, b_in),
                (grads_h.at[keep, :], own_g),
                (qacts_h, qacts),
                (eig_h, eig),
                (bout_h, b_out),
            )
        )
    ]
    l_back, l_deriv, l_acts, l_bin, l_own, l_qacts, l_eig, l_bout = loads
    l_top = pltpu.make_async_copy(qtop_h, errs, load_sem.at[len(loads)])

    @pl.when(seg == segs - 1)
    def _():
        l_top.start()

    for load in loads:
        load.start()
    own0 = pltpu.make_async_copy(
        grads_h.at[pl.ds(0, tb), cols(blk)], grads.at[0, mine0], g0_recv.at[0, lane]
    )
    own0.start()

    pl.semaphore_wait(barrier, blks - 1 + segs - 1)

    sel_a = remote(acts_h.at[give, :], other_a, sel_send.at[0], sel_recv.at[0], seg, mate)
    sel_a.start()
    sel_g = remote(grads_h.at[give, :], other_g, sel_send.at[1], sel_recv.at[1], seg, mate)
    sel_g.start()
    sends = [sel_a, sel_g]

    def to_chip(off):
        return lax.rem(chip + off, chips)

    def targets():
        for off in range(1, chips):
            for side in range(2):
                yield off, side, to_chip(off) * 2 + side
        yield 0, 0, mate

    for off, side, dest in targets():
        copy = remote(
            grads_h.at[pl.ds(0, tb), cols(dest)],
            grads.at[off, mine0],
            g0_send.at[off, side],
            g0_recv.at[off, lane],
            seg,
            dest,
        )
        copy.start()
        sends.append(copy)

    def e_copy(q):
        r = pl.ds(q * qt, qt)
        return remote(
            moved.at[r],
            errs.at[r],
            e_send.at[q],
            e_recv.at[q],
            lax.rem(seg + segs - 1, segs),
            blk,
        )

    def advance(q):
        r = pl.ds(q * qt, qt)
        e = errs[r]
        mixed = jnp.dot(e, back[...], preferred_element_type=F32)
        moved[r] = (e.astype(F32) + mixed * deriv[r].astype(F32)).astype(B16)
        e_copy(q).start()

    l_back.wait()
    l_deriv.wait()

    @pl.when(seg == segs - 1)
    def _():
        l_top.wait()
        for q in range(queries):
            advance(q)

    full = counts[blk] == SLOTS
    l_acts.wait()
    l_bin.wait()
    sel_a.wait_recv()
    racts[0, mine0] = jnp.dot(acts[0:tb], b_in[...], preferred_element_type=F32).astype(B16)
    picked = jnp.where(full, acts[keep, :].astype(F32), other_a[...].astype(F32)).astype(B16)
    racts[0, mine1] = jnp.dot(picked, b_in[...], preferred_element_type=F32).astype(B16)
    for off in list(range(1, chips)) + [0]:
        dest = mate if off == 0 else to_chip(off) * 2 + lane
        copy = remote(
            racts.at[0, mine], racts.at[off, mine], a_send.at[off], a_recv.at[off, lane], seg, dest
        )
        copy.start()
        sends.append(copy)

    l_own.wait()
    sel_g.wait_recv()
    own_g[...] = jnp.where(full, own_g[...].astype(F32), other_g[...].astype(F32)).astype(B16)
    for off, side, dest in targets():
        copy = remote(
            own_g.at[:, cols(dest)],
            grads.at[off, mine1],
            g1_send.at[off, side],
            g1_recv.at[off, lane],
            seg,
            dest,
        )
        copy.start()
        sends.append(copy)
    own1 = pltpu.make_async_copy(own_g.at[:, cols(blk)], grads.at[0, mine1], g1_recv.at[0, lane])
    own1.start()

    l_qacts.wait()
    rot_q[...] = jnp.dot(qacts[...], b_in[...], preferred_element_type=F32).astype(B16)
    l_eig.wait()
    inv[...] = 1.0 / (eig[...].astype(F32) + damping)
    l_bout.wait()

    @pl.when(jnp.logical_and(seg > 0, seg < segs - 1))
    def _():
        for q in range(queries):
            e_copy(q).wait_recv()
            advance(q)

    for off in range(1, chips):
        remote(
            racts.at[off, mine], racts.at[off, mine], f_send.at[off], a_recv.at[off, lane], seg, mate
        ).wait_recv()
        copy = remote(
            racts.at[off, mine], racts.at[off, mine], f_send.at[off], a_recv.at[off, lane], seg, mate
        )
        copy.start()
        sends.append(copy)

    @pl.when(seg == 0)
    def _():
        for q in range(queries):
            e_copy(q).wait_recv()

    rot_e = jnp.dot(errs[...], b_out[...], preferred_element_type=F32).astype(B16)
    for q in range(queries):
        raw = lax.dot_general(
            rot_e[q * qt : (q + 1) * qt],
            rot_q[q * qt : (q + 1) * qt, :],
            (((0,), (0,)), ((), ())),
            preferred_element_type=F32,
        )
        core_all[:, q * width : (q + 1) * width] = (raw * inv[...]).astype(B16)

    def group(i, carry):
        for side in range(2):
            for sem, size in ((g0_recv, tb), (g1_recv, half)):
                ref = grads.at[i, pl.ds(side * per + (tb if size == half else 0), size)]
                remote(ref, ref, g0_send.at[0, 0], sem.at[i, side], seg, mate).wait_recv()
        ref = racts.at[i, theirs]
        remote(ref, ref, f_send.at[0], a_recv.at[i, mate_lane], seg, mate).wait_recv()
        turned = jnp.dot(grads[i], b_out[...], preferred_element_type=F32).astype(B16)
        at = racts[i].astype(F32)
        for q in range(queries):
            h = jnp.dot(
                turned,
                core_all[:, q * width : (q + 1) * width],
                preferred_element_type=F32,
            )
            prod = h * at

            def small(x):
                x = jnp.sum(x, axis=0, keepdims=True)
                return sum(x[:, n * 128 : (n + 1) * 128] for n in range(width // 128))

            shared = small(prod[tb:per] + prod[per + tb : 2 * per])
            for side in range(2):
                part[i, side, q : q + 1, :] = small(prod[side * per : side * per + tb])
                part[i, side, queries + q : queries + q + 1, :] = shared
        return carry

    lax.fori_loop(0, chips, group, 0)

    def back_targets():
        for off in range(1, chips):
            for side in range(2):
                yield off, side, lax.rem(chip + chips - off, chips) * 2 + side

    for off, side, dest in back_targets():
        copy = remote(
            part.at[off, side],
            part_in.at[off, lane],
            p_send.at[off, side],
            p_recv.at[off, lane],
            seg,
            dest,
        )
        copy.start()
        sends.append(copy)
    copy = remote(
        part.at[0, mate_lane], part_in.at[0, lane], p_send.at[0, 0], p_recv.at[0, lane], seg, mate
    )
    copy.start()
    sends.append(copy)

    def p_wait(off, side):
        ref = part_in.at[off, side]
        remote(ref, ref, p_send.at[0, 0], p_recv.at[off, side], seg, mate).wait_recv()

    p_wait(0, mate_lane)
    total = part[0, lane] + part_in[0, mate_lane]
    for off in range(1, chips):
        for side in range(2):
            p_wait(off, side)
            total = total + part_in[off, side]
    zsum[seg] = total
    for off in range(1, segs):
        copy = remote(
            zsum.at[seg], zsum.at[seg], z_send.at[off], z_recv.at[seg], lax.rem(seg + off, segs), blk
        )
        copy.start()
        sends.append(copy)
    for off in range(1, segs):
        source = lax.rem(seg + off, segs)
        ref = zsum.at[source]
        remote(ref, ref, z_send.at[off], z_recv.at[source], source, blk).wait_recv()
    total = zsum[0]
    for n in range(1, segs):
        total = total + zsum[n]
    total = jnp.sum(total, axis=1, keepdims=True)
    out[:, 0:1] = total[0:queries]
    out[:, 1:2] = total[queries : 2 * queries] * jnp.where(full, 1.0, 0.0)

    for copy in sends:
        copy.wait_send()

    @pl.when(seg > 0)
    def _():
        for q in range(queries):
            e_copy(q).wait_send()


def body(
    train_acts,
    train_grads,
    counts,
    basis_in,
    basis_out,
    eigenvalues,
    back_weight,
    derivative,
    query_acts,
    query_top,
):
    segs = lax.axis_size("seg")
    blks = lax.axis_size("blk")
    chips = blks // 2
    queries, qt, width = query_top.shape
    rows = train_acts.shape[1]
    half = rows // SLOTS // 2
    per = rows // SLOTS + half
    wide = train_grads.shape[2]
    any_spec = pl.BlockSpec(memory_space=pl.ANY)
    vm = pltpu.VMEM
    dma = pltpu.SemaphoreType.DMA
    return pl.pallas_call(
        functools.partial(kernel, segs, blks, queries),
        out_shape=jax.ShapeDtypeStruct((queries, SLOTS), F32),
        in_specs=[pl.BlockSpec(memory_space=pltpu.SMEM)] + [any_spec] * 9,
        out_specs=pl.BlockSpec(memory_space=pltpu.VMEM),
        scratch_shapes=[
            vm((rows, width), B16),
            vm((half, wide), B16),
            vm((half, wide), B16),
            vm((half, width), B16),
            vm((width, width), B16),
            vm((width, width), B16),
            vm((width, width), B16),
            vm((width, width), B16),
            vm((queries * qt, width), B16),
            vm((queries * qt, width), B16),
            vm((queries * qt, width), B16),
            vm((queries * qt, width), B16),
            vm((width, width), F32),
            vm((queries * qt, width), B16),
            vm((width, queries * width), B16),
            vm((chips, 2 * per, width), B16),
            vm((chips, 2 * per, width), B16),
            vm((chips, 2, 2 * queries, 128), F32),
            vm((chips, 2, 2 * queries, 128), F32),
            vm((segs, 2 * queries, 128), F32),
            dma((9,)),
            dma((2,)),
            dma((2,)),
            dma((chips, 2)),
            dma((chips, 2)),
            dma((chips, 2)),
            dma((chips, 2)),
            dma((chips,)),
            dma((chips, 2)),
            dma((chips,)),
            dma((queries,)),
            dma((queries,)),
            dma((chips, 2)),
            dma((chips, 2)),
            dma((segs,)),
            dma((segs,)),
        ],
        compiler_params=pltpu.CompilerParams(
            collective_id=0, has_side_effects=True, vmem_limit_bytes=40 * 1024 * 1024
        ),
    )(
        counts,
        train_acts[0],
        train_grads[0],
        basis_in[0, 0],
        basis_out[0, 0],
        eigenvalues[0, 0],
        back_weight[0, 0],
        derivative[0].reshape(queries * qt, width),
        query_acts[0].reshape(queries * qt, width),
        query_top.reshape(queries * qt, width),
    )


def solution(mesh):
    in_specs = (
        P("seg", "blk", None),
        P("seg", "blk", None),
        P(),
        P("seg", None, None, None),
        P("seg", "blk", None, None),
        P("seg", "blk", None, None),
        P("seg", "blk", None, None),
        P("seg", None, None, "blk"),
        P("seg", None, None, None),
        P(None, None, "blk"),
    )
    out_specs = P(None, "blk")
    return jax.shard_map(body, mesh=mesh, in_specs=in_specs, out_specs=out_specs, check_vma=False)
```

```python
import functools

import jax
import jax.numpy as jnp
from jax import lax
from jax.experimental import pallas as pl
from jax.experimental.pallas import tpu as pltpu
from jax.sharding import PartitionSpec as P

SLOTS = 2
damping = 0.05
F32 = jnp.float32
B16 = jnp.bfloat16
MESH = pl.DeviceIdType.MESH


def kernel(
    segs,
    blks,
    queries,
    counts,
    acts_h,
    grads_h,
    bin_h,
    bout_h,
    eig_h,
    back_h,
    deriv_h,
    qacts_h,
    qtop_h,
    out,
    acts,
    own_g,
    other_g,
    other_a,
    b_in,
    b_out,
    eig,
    back,
    deriv,
    qacts,
    errs,
    moved,
    inv,
    rot_q,
    core_all,
    grads,
    racts,
    part,
    part_in,
    zsum,
    load_sem,
    sel_send,
    sel_recv,
    g0_send,
    g0_recv,
    g1_send,
    g1_recv,
    a_send,
    a_recv,
    f_send,
    e_send,
    e_recv,
    p_send,
    p_recv,
    z_send,
    z_recv,
):
    seg = lax.axis_index("seg")
    blk = lax.axis_index("blk")
    chips = blks // 2
    chip = blk // 2
    lane = blk % 2
    mate_lane = 1 - lane
    mate = chip * 2 + mate_lane
    rows = acts_h.shape[0]
    tb = rows // SLOTS
    half = tb // 2
    per = tb + half
    width = bin_h.shape[0]
    qt = qtop_h.shape[0] // queries

    def remote(src, dst, ssem, rsem, seg_to, blk_to):
        return pltpu.make_async_remote_copy(
            src_ref=src,
            dst_ref=dst,
            send_sem=ssem,
            recv_sem=rsem,
            device_id=(seg_to, blk_to),
            device_id_type=MESH,
        )

    def cols(index):
        return pl.ds(pl.multiple_of(index * width, width), width)

    barrier = pltpu.get_barrier_semaphore()
    for off in range(1, blks):
        pl.semaphore_signal(
            barrier, inc=1, device_id=(seg, lax.rem(blk + off, blks)), device_id_type=MESH
        )
    for off in range(1, segs):
        pl.semaphore_signal(
            barrier, inc=1, device_id=(lax.rem(seg + off, segs), blk), device_id_type=MESH
        )

    keep = pl.ds(pl.multiple_of(tb + lane * half, half), half)
    give = pl.ds(pl.multiple_of(tb + mate_lane * half, half), half)
    mine0 = pl.ds(pl.multiple_of(lane * per, half), tb)
    mine1 = pl.ds(pl.multiple_of(lane * per + tb, half), half)
    mine = pl.ds(pl.multiple_of(lane * per, half), per)
    theirs = pl.ds(pl.multiple_of(mate_lane * per, half), per)

    loads = [
        pltpu.make_async_copy(src, dst, load_sem.at[n])
        for n, (src, dst) in enumerate(
            (
                (back_h, back),
                (deriv_h, deriv),
                (acts_h, acts),
                (bin_h, b_in),
                (grads_h.at[keep, :], own_g),
                (qacts_h, qacts),
                (eig_h, eig),
                (bout_h, b_out),
            )
        )
    ]
    l_back, l_deriv, l_acts, l_bin, l_own, l_qacts, l_eig, l_bout = loads
    l_top = pltpu.make_async_copy(qtop_h, errs, load_sem.at[len(loads)])

    @pl.when(seg == segs - 1)
    def _():
        l_top.start()

    for load in loads:
        load.start()
    own0 = pltpu.make_async_copy(
        grads_h.at[pl.ds(0, tb), cols(blk)], grads.at[0, mine0], g0_recv.at[0, lane]
    )
    own0.start()

    pl.semaphore_wait(barrier, blks - 1 + segs - 1)

    sel_a = remote(acts_h.at[give, :], other_a, sel_send.at[0], sel_recv.at[0], seg, mate)
    sel_a.start()
    sel_g = remote(grads_h.at[give, :], other_g, sel_send.at[1], sel_recv.at[1], seg, mate)
    sel_g.start()
    sends = [sel_a, sel_g]

    def to_chip(off):
        return lax.rem(chip + off, chips)

    def targets():
        for off in range(1, chips):
            for side in range(2):
                yield off, side, to_chip(off) * 2 + side
        yield 0, 0, mate

    for off, side, dest in targets():
        copy = remote(
            grads_h.at[pl.ds(0, tb), cols(dest)],
            grads.at[off, mine0],
            g0_send.at[off, side],
            g0_recv.at[off, lane],
            seg,
            dest,
        )
        copy.start()
        sends.append(copy)

    def e_copy(q):
        r = pl.ds(q * qt, qt)
        return remote(
            moved.at[r],
            errs.at[r],
            e_send.at[q],
            e_recv.at[q],
            lax.rem(seg + segs - 1, segs),
            blk,
        )

    def advance(q):
        r = pl.ds(q * qt, qt)
        e = errs[r]
        mixed = jnp.dot(e, back[...], preferred_element_type=F32)
        moved[r] = (e.astype(F32) + mixed * deriv[r].astype(F32)).astype(B16)
        e_copy(q).start()

    l_back.wait()
    l_deriv.wait()

    @pl.when(seg == segs - 1)
    def _():
        l_top.wait()
        for q in range(queries):
            advance(q)

    full = counts[blk] == SLOTS
    l_acts.wait()
    l_bin.wait()
    sel_a.wait_recv()
    racts[0, mine0] = jnp.dot(acts[0:tb], b_in[...], preferred_element_type=F32).astype(B16)
    picked = jnp.where(full, acts[keep, :].astype(F32), other_a[...].astype(F32)).astype(B16)
    racts[0, mine1] = jnp.dot(picked, b_in[...], preferred_element_type=F32).astype(B16)
    for off in list(range(1, chips)) + [0]:
        dest = mate if off == 0 else to_chip(off) * 2 + lane
        copy = remote(
            racts.at[0, mine], racts.at[off, mine], a_send.at[off], a_recv.at[off, lane], seg, dest
        )
        copy.start()
        sends.append(copy)

    l_own.wait()
    sel_g.wait_recv()
    own_g[...] = jnp.where(full, own_g[...].astype(F32), other_g[...].astype(F32)).astype(B16)
    for off, side, dest in targets():
        copy = remote(
            own_g.at[:, cols(dest)],
            grads.at[off, mine1],
            g1_send.at[off, side],
            g1_recv.at[off, lane],
            seg,
            dest,
        )
        copy.start()
        sends.append(copy)
    own1 = pltpu.make_async_copy(own_g.at[:, cols(blk)], grads.at[0, mine1], g1_recv.at[0, lane])
    own1.start()

    l_qacts.wait()
    rot_q[...] = jnp.dot(qacts[...], b_in[...], preferred_element_type=F32).astype(B16)
    l_eig.wait()
    inv[...] = 1.0 / (eig[...].astype(F32) + damping)
    l_bout.wait()

    @pl.when(jnp.logical_and(seg > 0, seg < segs - 1))
    def _():
        for q in range(queries):
            e_copy(q).wait_recv()
            advance(q)

    for off in range(1, chips):
        remote(
            racts.at[off, mine], racts.at[off, mine], f_send.at[off], a_recv.at[off, lane], seg, mate
        ).wait_recv()
        copy = remote(
            racts.at[off, mine], racts.at[off, mine], f_send.at[off], a_recv.at[off, lane], seg, mate
        )
        copy.start()
        sends.append(copy)

    @pl.when(seg == 0)
    def _():
        for q in range(queries):
            e_copy(q).wait_recv()

    rot_e = jnp.dot(errs[...], b_out[...], preferred_element_type=F32).astype(B16)
    for q in range(queries):
        raw = lax.dot_general(
            rot_e[q * qt : (q + 1) * qt],
            rot_q[q * qt : (q + 1) * qt, :],
            (((0,), (0,)), ((), ())),
            preferred_element_type=F32,
        )
        core_all[:, q * width : (q + 1) * width] = (raw * inv[...]).astype(B16)

    def group(i, carry):
        for side in range(2):
            for sem, size in ((g0_recv, tb), (g1_recv, half)):
                ref = grads.at[i, pl.ds(side * per + (tb if size == half else 0), size)]
                remote(ref, ref, g0_send.at[0, 0], sem.at[i, side], seg, mate).wait_recv()
        ref = racts.at[i, theirs]
        remote(ref, ref, f_send.at[0], a_recv.at[i, mate_lane], seg, mate).wait_recv()
        turned = jnp.dot(grads[i], b_out[...], preferred_element_type=F32).astype(B16)
        at = racts[i].astype(F32)
        for q in range(queries):
            h = jnp.dot(
                turned,
                core_all[:, q * width : (q + 1) * width],
                preferred_element_type=F32,
            )
            prod = h * at

            def small(x):
                x = jnp.sum(x, axis=0, keepdims=True)
                return sum(x[:, n * 128 : (n + 1) * 128] for n in range(width // 128))

            shared = small(prod[tb:per] + prod[per + tb : 2 * per])
            for side in range(2):
                part[i, side, q : q + 1, :] = small(prod[side * per : side * per + tb])
                part[i, side, queries + q : queries + q + 1, :] = shared
        return carry

    lax.fori_loop(0, chips, group, 0)

    def back_targets():
        for off in range(1, chips):
            for side in range(2):
                yield off, side, lax.rem(chip + chips - off, chips) * 2 + side

    for off, side, dest in back_targets():
        copy = remote(
            part.at[off, side],
            part_in.at[off, lane],
            p_send.at[off, side],
            p_recv.at[off, lane],
            seg,
            dest,
        )
        copy.start()
        sends.append(copy)
    copy = remote(
        part.at[0, mate_lane], part_in.at[0, lane], p_send.at[0, 0], p_recv.at[0, lane], seg, mate
    )
    copy.start()
    sends.append(copy)

    def p_wait(off, side):
        ref = part_in.at[off, side]
        remote(ref, ref, p_send.at[0, 0], p_recv.at[off, side], seg, mate).wait_recv()

    p_wait(0, mate_lane)
    total = part[0, lane] + part_in[0, mate_lane]
    for off in range(1, chips):
        for side in range(2):
            p_wait(off, side)
            total = total + part_in[off, side]
    zsum[seg] = total
    for off in range(1, segs):
        copy = remote(
            zsum.at[seg], zsum.at[seg], z_send.at[off], z_recv.at[seg], lax.rem(seg + off, segs), blk
        )
        copy.start()
        sends.append(copy)
    for off in range(1, segs):
        source = lax.rem(seg + off, segs)
        ref = zsum.at[source]
        remote(ref, ref, z_send.at[off], z_recv.at[source], source, blk).wait_recv()
    total = zsum[0]
    for n in range(1, segs):
        total = total + zsum[n]
    total = jnp.sum(total, axis=1, keepdims=True)
    out[:, 0:1] = total[0:queries]
    out[:, 1:2] = total[queries : 2 * queries] * jnp.where(full, 1.0, 0.0)

    for copy in sends:
        copy.wait_send()

    @pl.when(seg > 0)
    def _():
        for q in range(queries):
            e_copy(q).wait_send()


def body(
    train_acts,
    train_grads,
    counts,
    basis_in,
    basis_out,
    eigenvalues,
    back_weight,
    derivative,
    query_acts,
    query_top,
):
    segs = lax.axis_size("seg")
    blks = lax.axis_size("blk")
    chips = blks // 2
    queries, qt, width = query_top.shape
    rows = train_acts.shape[1]
    half = rows // SLOTS // 2
    per = rows // SLOTS + half
    wide = train_grads.shape[2]
    any_spec = pl.BlockSpec(memory_space=pltpu.HBM)
    vm = pltpu.VMEM
    dma = pltpu.SemaphoreType.DMA
    return pl.pallas_call(
        functools.partial(kernel, segs, blks, queries),
        out_shape=jax.ShapeDtypeStruct((queries, SLOTS), F32),
        in_specs=[pl.BlockSpec(memory_space=pltpu.SMEM)] + [any_spec] * 9,
        out_specs=pl.BlockSpec(memory_space=pltpu.VMEM),
        scratch_shapes=[
            vm((rows, width), B16),
            vm((half, wide), B16),
            vm((half, wide), B16),
            vm((half, width), B16),
            vm((width, width), B16),
            vm((width, width), B16),
            vm((width, width), B16),
            vm((width, width), B16),
            vm((queries * qt, width), B16),
            vm((queries * qt, width), B16),
            vm((queries * qt, width), B16),
            vm((queries * qt, width), B16),
            vm((width, width), F32),
            vm((queries * qt, width), B16),
            vm((width, queries * width), B16),
            vm((chips, 2 * per, width), B16),
            vm((chips, 2 * per, width), B16),
            vm((chips, 2, 2 * queries, 128), F32),
            vm((chips, 2, 2 * queries, 128), F32),
            vm((segs, 2 * queries, 128), F32),
            dma((9,)),
            dma((2,)),
            dma((2,)),
            dma((chips, 2)),
            dma((chips, 2)),
            dma((chips, 2)),
            dma((chips, 2)),
            dma((chips,)),
            dma((chips, 2)),
            dma((chips,)),
            dma((queries,)),
            dma((queries,)),
            dma((chips, 2)),
            dma((chips, 2)),
            dma((segs,)),
            dma((segs,)),
        ],
        compiler_params=pltpu.CompilerParams(
            collective_id=0, has_side_effects=True, vmem_limit_bytes=67_043_328
        ),
    )(
        counts,
        train_acts[0],
        train_grads[0],
        basis_in[0, 0],
        basis_out[0, 0],
        eigenvalues[0, 0],
        back_weight[0, 0],
        derivative[0].reshape(queries * qt, width),
        query_acts[0].reshape(queries * qt, width),
        query_top.reshape(queries * qt, width),
    )


def solution(mesh):
    in_specs = (
        P("seg", "blk", None),
        P("seg", "blk", None),
        P(),
        P("seg", None, None, None),
        P("seg", "blk", None, None),
        P("seg", "blk", None, None),
        P("seg", "blk", None, None),
        P("seg", None, None, "blk"),
        P("seg", None, None, None),
        P(None, None, "blk"),
    )
    out_specs = P(None, "blk")
    return jax.shard_map(body, mesh=mesh, in_specs=in_specs, out_specs=out_specs, check_vma=False)
```

```python
import functools

import jax
import jax.numpy as jnp
from jax import lax
from jax.experimental import pallas as pl
from jax.experimental.pallas import tpu as pltpu
from jax.sharding import PartitionSpec as P

SLOTS = 2
damping = 0.05
F32 = jnp.float32
B16 = jnp.bfloat16
MESH = pl.DeviceIdType.MESH


def kernel(
    segs,
    blks,
    queries,
    counts,
    acts_h,
    grads_h,
    bin_h,
    bout_h,
    eig_h,
    back_h,
    deriv_h,
    qacts_h,
    qtop_h,
    out,
    acts,
    own_g,
    other_g,
    other_a,
    b_in,
    b_out,
    eig,
    back,
    deriv,
    qacts,
    errs,
    moved,
    inv,
    rot_q,
    core_all,
    grads0,
    grads1,
    racts0,
    racts1,
    turned0,
    part,
    packed,
    gathered,
    load_sem,
    sel_send,
    sel_recv,
    g0_send,
    g0_recv,
    g1_send,
    g1_recv,
    a0_send,
    a0_recv,
    a1_send,
    a1_recv,
    f0_send,
    f1_send,
    e_send,
    e_recv,
    p_send,
    p_recv,
    ready,
):
    seg = lax.axis_index("seg")
    blk = lax.axis_index("blk")
    chips = blks // 2
    chip = blk // 2
    lane = blk % 2
    mate_lane = 1 - lane
    mate = chip * 2 + mate_lane
    rows = acts_h.shape[0]
    tb = rows // SLOTS
    half = tb // 2
    width = bin_h.shape[0]
    qt = qtop_h.shape[0] // queries

    def remote(src, dst, ssem, rsem, seg_to, blk_to):
        return pltpu.make_async_remote_copy(
            src_ref=src,
            dst_ref=dst,
            send_sem=ssem,
            recv_sem=rsem,
            device_id=(seg_to, blk_to),
            device_id_type=MESH,
        )

    def cols(index):
        return pl.ds(pl.multiple_of(index * width, width), width)

    barrier = pltpu.get_barrier_semaphore()
    for off in range(1, blks):
        pl.semaphore_signal(
            barrier, inc=1, device_id=(seg, lax.rem(blk + off, blks)), device_id_type=MESH
        )
    for off in range(1, segs):
        pl.semaphore_signal(
            barrier, inc=1, device_id=(lax.rem(seg + off, segs), blk), device_id_type=MESH
        )

    keep = pl.ds(pl.multiple_of(tb + lane * half, half), half)
    give = pl.ds(pl.multiple_of(tb + mate_lane * half, half), half)
    mine0 = pl.ds(pl.multiple_of(lane * tb, tb), tb)
    mine1 = pl.ds(pl.multiple_of(lane * half, half), half)

    loads = [
        pltpu.make_async_copy(src, dst, load_sem.at[n])
        for n, (src, dst) in enumerate(
            (
                (back_h, back),
                (deriv_h, deriv),
                (acts_h, acts),
                (bin_h, b_in),
                (grads_h.at[keep, :], own_g),
                (qacts_h, qacts),
                (eig_h, eig),
                (bout_h, b_out),
            )
        )
    ]
    l_back, l_deriv, l_acts, l_bin, l_own, l_qacts, l_eig, l_bout = loads
    l_top = pltpu.make_async_copy(qtop_h, errs, load_sem.at[len(loads)])

    @pl.when(seg == segs - 1)
    def _():
        l_top.start()

    for load in loads:
        load.start()
    own0 = pltpu.make_async_copy(
        grads_h.at[pl.ds(0, tb), cols(blk)], grads0.at[0, mine0], g0_recv.at[0, lane]
    )
    own0.start()

    def e_copy(q):
        r = pl.ds(q * qt, qt)
        return remote(
            moved.at[r],
            errs.at[r],
            e_send.at[q],
            e_recv.at[q],
            lax.rem(seg + segs - 1, segs),
            blk,
        )

    def advance(q):
        r = pl.ds(q * qt, qt)
        e = errs[r]
        mixed = jnp.dot(e, back[...], preferred_element_type=F32)
        moved[r] = (e.astype(F32) + mixed * deriv[r].astype(F32)).astype(B16)

    l_back.wait()
    l_deriv.wait()

    @pl.when(seg == segs - 1)
    def _():
        l_top.wait()
        for q in range(queries):
            advance(q)

    l_acts.wait()
    l_bin.wait()
    racts0[0, mine0] = jnp.dot(acts[0:tb], b_in[...], preferred_element_type=F32).astype(B16)

    pl.semaphore_wait(barrier, blks - 1 + segs - 1)

    @pl.when(seg == segs - 1)
    def _():
        for q in range(queries):
            e_copy(q).start()

    sends = []

    def send(copy):
        copy.start()
        sends.append(copy)
        return copy

    sel_a = send(remote(acts_h.at[give, :], other_a, sel_send.at[0], sel_recv.at[0], seg, mate))
    sel_g = send(remote(grads_h.at[give, :], other_g, sel_send.at[1], sel_recv.at[1], seg, mate))

    def to_chip(off):
        return lax.rem(chip + off, chips)

    def targets():
        for off in range(1, chips):
            for side in range(2):
                yield off, side, to_chip(off) * 2 + side
        yield 0, 0, mate

    def act_targets():
        for off in range(1, chips):
            yield off, to_chip(off) * 2 + lane
        yield 0, mate

    for off, side, dest in targets():
        send(
            remote(
                grads_h.at[pl.ds(0, tb), cols(dest)],
                grads0.at[off, mine0],
                g0_send.at[off, side],
                g0_recv.at[off, lane],
                seg,
                dest,
            )
        )
    for off, dest in act_targets():
        send(
            remote(
                racts0.at[0, mine0],
                racts0.at[off, mine0],
                a0_send.at[off],
                a0_recv.at[off, lane],
                seg,
                dest,
            )
        )
    for off in range(1, segs):
        pl.semaphore_signal(
            ready, inc=1, device_id=(lax.rem(seg + off, segs), blk), device_id_type=MESH
        )

    full = counts[blk] == SLOTS
    sel_a.wait_recv()
    picked = jnp.where(full, acts[keep, :].astype(F32), other_a[...].astype(F32)).astype(B16)
    racts1[0, mine1] = jnp.dot(picked, b_in[...], preferred_element_type=F32).astype(B16)
    for off, dest in act_targets():
        send(
            remote(
                racts1.at[0, mine1],
                racts1.at[off, mine1],
                a1_send.at[off],
                a1_recv.at[off, lane],
                seg,
                dest,
            )
        )

    l_own.wait()
    sel_g.wait_recv()
    own_g[...] = jnp.where(full, own_g[...].astype(F32), other_g[...].astype(F32)).astype(B16)
    for off, side, dest in targets():
        send(
            remote(
                own_g.at[:, cols(dest)],
                grads1.at[off, mine1],
                g1_send.at[off, side],
                g1_recv.at[off, lane],
                seg,
                dest,
            )
        )
    own1 = pltpu.make_async_copy(own_g.at[:, cols(blk)], grads1.at[0, mine1], g1_recv.at[0, lane])
    own1.start()

    l_qacts.wait()
    rot_q[...] = jnp.dot(qacts[...], b_in[...], preferred_element_type=F32).astype(B16)
    l_eig.wait()
    inv[...] = 1.0 / (eig[...].astype(F32) + damping)
    l_bout.wait()

    @pl.when(jnp.logical_and(seg > 0, seg < segs - 1))
    def _():
        for q in range(queries):
            e_copy(q).wait_recv()
            advance(q)
            e_copy(q).start()

    def arrived(buf, sem, i, side, size):
        ref = buf.at[i, pl.ds(pl.multiple_of(side * size, size), size)]
        remote(ref, ref, sel_send.at[0], sem.at[i, side], seg, mate).wait_recv()

    for buf, sem, fsem, rows_of, size in (
        (racts0, a0_recv, f0_send, mine0, tb),
        (racts1, a1_recv, f1_send, mine1, half),
    ):
        for off in range(1, chips):
            arrived(buf, sem, off, lane, size)
            ref = buf.at[off, rows_of]
            send(remote(ref, ref, fsem.at[off], sem.at[off, lane], seg, mate))

    for i in range(chips):
        for side in range(2):
            arrived(grads0, g0_recv, i, side, tb)
        turned0[i] = jnp.dot(grads0[i], b_out[...], preferred_element_type=F32).astype(B16)
    for i in range(chips):
        arrived(racts0, a0_recv, i, mate_lane, tb)

    def core_of(q):
        return core_all[:, q * width : (q + 1) * width]

    def folded(x):
        x = sum(x[:, n * 128 : (n + 1) * 128] for n in range(width // 128))
        return jnp.sum(x, axis=0, keepdims=True)

    for q in range(queries):

        @pl.when(seg == 0)
        def _():
            e_copy(q).wait_recv()

        r = pl.ds(q * qt, qt)
        rot_e = jnp.dot(errs[r], b_out[...], preferred_element_type=F32).astype(B16)
        raw = lax.dot_general(
            rot_e, rot_q[r], (((0,), (0,)), ((), ())), preferred_element_type=F32
        )
        core_all[:, q * width : (q + 1) * width] = (raw * inv[...]).astype(B16)
        for i in range(chips):
            h = jnp.dot(turned0[i], core_of(q), preferred_element_type=F32)
            prod = h * racts0[i].astype(F32)
            for side in range(2):
                part[i, side, q : q + 1, :] = folded(prod[side * tb : (side + 1) * tb])

    for i in range(chips):
        for side in range(2):
            arrived(grads1, g1_recv, i, side, half)
        arrived(racts1, a1_recv, i, mate_lane, half)
    late = jnp.dot(
        grads1[...].reshape(chips * tb, width), b_out[...], preferred_element_type=F32
    ).astype(B16)
    for q in range(queries):
        h = jnp.dot(late, core_of(q), preferred_element_type=F32)
        prod = h * racts1[...].reshape(chips * tb, width).astype(F32)
        for i in range(chips):
            shared = folded(prod[i * tb : (i + 1) * tb])
            for side in range(2):
                part[i, side, queries + q : queries + q + 1, :] = shared

    values = 2 * queries
    tile = (chips, 2, values, 128)
    diag = lax.broadcasted_iota(jnp.int32, tile, 2) == lax.broadcasted_iota(jnp.int32, tile, 3)
    sums = jnp.sum(part[...], axis=3, keepdims=True)
    packed[...] = jnp.sum(jnp.where(diag, sums, 0.0), axis=2, keepdims=True)

    pl.semaphore_wait(ready, segs - 1)
    for seg_off in range(segs - 1, -1, -1):
        seg_to = lax.rem(seg + seg_off, segs)
        for off in range(chips):
            chip_to = lax.rem(chip + chips - off, chips)
            for turn in range(2):
                if seg_off == 0 and off == 0 and turn == 0:
                    continue
                side = lane if turn == 0 else mate_lane
                send(
                    remote(
                        packed.at[off, side],
                        gathered.at[seg, blk],
                        p_send.at[seg_off, off, turn],
                        p_recv.at[seg, blk],
                        seg_to,
                        chip_to * 2 + side,
                    )
                )
    gathered[seg, blk] = packed[0, lane]
    for seg_off in range(segs):
        for off in range(blks):
            if seg_off == 0 and off == 0:
                continue
            a, b = lax.rem(seg + seg_off, segs), lax.rem(blk + off, blks)
            ref = gathered.at[a, b]
            remote(ref, ref, sel_send.at[0], p_recv.at[a, b], seg, mate).wait_recv()
    total = jnp.sum(gathered[...].reshape(segs * blks, 128), axis=0, keepdims=True)
    tile = (values, 128)
    diag = lax.broadcasted_iota(jnp.int32, tile, 0) == lax.broadcasted_iota(jnp.int32, tile, 1)
    total = jnp.sum(jnp.where(diag, jnp.broadcast_to(total, tile), 0.0), axis=1, keepdims=True)
    out[:, 0:1] = total[0:queries]
    out[:, 1:2] = total[queries:values] * jnp.where(full, 1.0, 0.0)

    for copy in sends:
        copy.wait_send()

    @pl.when(seg > 0)
    def _():
        for q in range(queries):
            e_copy(q).wait_send()


def body(
    train_acts,
    train_grads,
    counts,
    basis_in,
    basis_out,
    eigenvalues,
    back_weight,
    derivative,
    query_acts,
    query_top,
):
    segs = lax.axis_size("seg")
    blks = lax.axis_size("blk")
    chips = blks // 2
    queries, qt, width = query_top.shape
    rows = train_acts.shape[1]
    tb = rows // SLOTS
    half = tb // 2
    wide = train_grads.shape[2]
    any_spec = pl.BlockSpec(memory_space=pltpu.HBM)
    vm = pltpu.VMEM
    dma = pltpu.SemaphoreType.DMA
    return pl.pallas_call(
        functools.partial(kernel, segs, blks, queries),
        out_shape=jax.ShapeDtypeStruct((queries, SLOTS), F32),
        in_specs=[pl.BlockSpec(memory_space=pltpu.SMEM)] + [any_spec] * 9,
        out_specs=pl.BlockSpec(memory_space=pltpu.VMEM),
        scratch_shapes=[
            vm((rows, width), B16),
            vm((half, wide), B16),
            vm((half, wide), B16),
            vm((half, width), B16),
            vm((width, width), B16),
            vm((width, width), B16),
            vm((width, width), B16),
            vm((width, width), B16),
            vm((queries * qt, width), B16),
            vm((queries * qt, width), B16),
            vm((queries * qt, width), B16),
            vm((queries * qt, width), B16),
            vm((width, width), F32),
            vm((queries * qt, width), B16),
            vm((width, queries * width), B16),
            vm((chips, 2 * tb, width), B16),
            vm((chips, 2 * half, width), B16),
            vm((chips, 2 * tb, width), B16),
            vm((chips, 2 * half, width), B16),
            vm((chips, 2 * tb, width), B16),
            vm((chips, 2, 2 * queries, 128), F32),
            vm((chips, 2, 1, 128), F32),
            vm((segs, blks, 1, 128), F32),
            dma((9,)),
            dma((2,)),
            dma((2,)),
            dma((chips, 2)),
            dma((chips, 2)),
            dma((chips, 2)),
            dma((chips, 2)),
            dma((chips,)),
            dma((chips, 2)),
            dma((chips,)),
            dma((chips, 2)),
            dma((chips,)),
            dma((chips,)),
            dma((queries,)),
            dma((queries,)),
            dma((segs, chips, 2)),
            dma((segs, blks)),
            pltpu.SemaphoreType.REGULAR,
        ],
        compiler_params=pltpu.CompilerParams(
            collective_id=0, has_side_effects=True, vmem_limit_bytes=67_043_328
        ),
    )(
        counts,
        train_acts[0],
        train_grads[0],
        basis_in[0, 0],
        basis_out[0, 0],
        eigenvalues[0, 0],
        back_weight[0, 0],
        derivative[0].reshape(queries * qt, width),
        query_acts[0].reshape(queries * qt, width),
        query_top.reshape(queries * qt, width),
    )


def solution(mesh):
    in_specs = (
        P("seg", "blk", None),
        P("seg", "blk", None),
        P(),
        P("seg", None, None, None),
        P("seg", "blk", None, None),
        P("seg", "blk", None, None),
        P("seg", "blk", None, None),
        P("seg", None, None, "blk"),
        P("seg", None, None, None),
        P(None, None, "blk"),
    )
    out_specs = P(None, "blk")
    return jax.shard_map(body, mesh=mesh, in_specs=in_specs, out_specs=out_specs, check_vma=False)
```

```python
import functools

import jax
import jax.numpy as jnp
from jax import lax
from jax.experimental import pallas as pl
from jax.experimental.pallas import tpu as pltpu
from jax.sharding import PartitionSpec as P

SLOTS = 2
damping = 0.05
F32 = jnp.float32
B16 = jnp.bfloat16
MESH = pl.DeviceIdType.MESH


def kernel(
    segs,
    blks,
    queries,
    counts,
    acts_h,
    grads_h,
    bin_h,
    bout_h,
    eig_h,
    back_h,
    deriv_h,
    qacts_h,
    qtop_h,
    out,
    acts,
    own_g,
    other_g,
    other_a,
    b_in,
    b_out,
    eig,
    back,
    deriv,
    qacts,
    errs,
    moved,
    inv,
    rot_q,
    core_all,
    grads0,
    grads1,
    racts0,
    racts1,
    turned0,
    part,
    packed,
    gathered,
    load_sem,
    sel_send,
    sel_recv,
    g0_send,
    g0_recv,
    g1_send,
    g1_recv,
    a0_send,
    a0_recv,
    a1_send,
    a1_recv,
    f0_send,
    f1_send,
    e_send,
    e_recv,
    p_send,
    p_recv,
    ready,
):
    seg = lax.axis_index("seg")
    blk = lax.axis_index("blk")
    chips = blks // 2
    chip = blk // 2
    lane = blk % 2
    mate_lane = 1 - lane
    mate = chip * 2 + mate_lane
    rows = acts_h.shape[0]
    tb = rows // SLOTS
    half = tb // 2
    width = bin_h.shape[0]
    qt = qtop_h.shape[0] // queries

    def remote(src, dst, ssem, rsem, seg_to, blk_to):
        return pltpu.make_async_remote_copy(
            src_ref=src,
            dst_ref=dst,
            send_sem=ssem,
            recv_sem=rsem,
            device_id=(seg_to, blk_to),
            device_id_type=MESH,
        )

    def cols(index):
        return pl.ds(pl.multiple_of(index * width, width), width)

    barrier = pltpu.get_barrier_semaphore()
    for off in range(1, blks):
        pl.semaphore_signal(
            barrier, inc=1, device_id=(seg, lax.rem(blk + off, blks)), device_id_type=MESH
        )
    for off in range(1, segs):
        pl.semaphore_signal(
            barrier, inc=1, device_id=(lax.rem(seg + off, segs), blk), device_id_type=MESH
        )

    keep = pl.ds(pl.multiple_of(tb + lane * half, half), half)
    give = pl.ds(pl.multiple_of(tb + mate_lane * half, half), half)
    mine0 = pl.ds(pl.multiple_of(lane * tb, tb), tb)
    mine1 = pl.ds(pl.multiple_of(lane * half, half), half)

    loads = [
        pltpu.make_async_copy(src, dst, load_sem.at[n])
        for n, (src, dst) in enumerate(
            (
                (back_h, back),
                (deriv_h, deriv),
                (acts_h, acts),
                (bin_h, b_in),
                (grads_h.at[keep, :], own_g),
                (qacts_h, qacts),
                (eig_h, eig),
                (bout_h, b_out),
            )
        )
    ]
    l_back, l_deriv, l_acts, l_bin, l_own, l_qacts, l_eig, l_bout = loads
    l_top = pltpu.make_async_copy(qtop_h, errs, load_sem.at[len(loads)])

    @pl.when(seg == segs - 1)
    def _():
        l_top.start()

    for load in loads:
        load.start()
    own0 = pltpu.make_async_copy(
        grads_h.at[pl.ds(0, tb), cols(blk)], grads0.at[0, mine0], g0_recv.at[0, lane]
    )
    own0.start()

    def e_copy(q):
        r = pl.ds(q * qt, qt)
        return remote(
            moved.at[r],
            errs.at[r],
            e_send.at[q],
            e_recv.at[q],
            lax.rem(seg + segs - 1, segs),
            blk,
        )

    def advance(q):
        r = pl.ds(q * qt, qt)
        e = errs[r]
        mixed = jnp.dot(e, back[...], preferred_element_type=F32)
        moved[r] = (e.astype(F32) + mixed * deriv[r].astype(F32)).astype(B16)

    l_back.wait()
    l_deriv.wait()

    @pl.when(seg == segs - 1)
    def _():
        l_top.wait()
        for q in range(queries):
            advance(q)

    pl.semaphore_wait(barrier, blks - 1 + segs - 1)

    @pl.when(seg == segs - 1)
    def _():
        for q in range(queries):
            e_copy(q).start()

    sends = []

    def send(copy):
        copy.start()
        sends.append(copy)
        return copy

    sel_a = send(remote(acts_h.at[give, :], other_a, sel_send.at[0], sel_recv.at[0], seg, mate))
    sel_g = send(remote(grads_h.at[give, :], other_g, sel_send.at[1], sel_recv.at[1], seg, mate))

    def to_chip(off):
        return lax.rem(chip + off, chips)

    def targets():
        for off in range(1, chips):
            for side in range(2):
                yield off, side, to_chip(off) * 2 + side
        yield 0, 0, mate

    def act_targets():
        for off in range(1, chips):
            yield off, to_chip(off) * 2 + lane
        yield 0, mate

    for off, side, dest in targets():
        send(
            remote(
                grads_h.at[pl.ds(0, tb), cols(dest)],
                grads0.at[off, mine0],
                g0_send.at[off, side],
                g0_recv.at[off, lane],
                seg,
                dest,
            )
        )
    l_acts.wait()
    l_bin.wait()
    racts0[0, mine0] = jnp.dot(acts[0:tb], b_in[...], preferred_element_type=F32).astype(B16)

    for off, dest in act_targets():
        send(
            remote(
                racts0.at[0, mine0],
                racts0.at[off, mine0],
                a0_send.at[off],
                a0_recv.at[off, lane],
                seg,
                dest,
            )
        )
    for off in range(1, segs):
        pl.semaphore_signal(
            ready, inc=1, device_id=(lax.rem(seg + off, segs), blk), device_id_type=MESH
        )

    full = counts[blk] == SLOTS
    sel_a.wait_recv()
    picked = jnp.where(full, acts[keep, :].astype(F32), other_a[...].astype(F32)).astype(B16)
    racts1[0, mine1] = jnp.dot(picked, b_in[...], preferred_element_type=F32).astype(B16)
    for off, dest in act_targets():
        send(
            remote(
                racts1.at[0, mine1],
                racts1.at[off, mine1],
                a1_send.at[off],
                a1_recv.at[off, lane],
                seg,
                dest,
            )
        )

    l_own.wait()
    sel_g.wait_recv()
    own_g[...] = jnp.where(full, own_g[...].astype(F32), other_g[...].astype(F32)).astype(B16)
    for off, side, dest in targets():
        send(
            remote(
                own_g.at[:, cols(dest)],
                grads1.at[off, mine1],
                g1_send.at[off, side],
                g1_recv.at[off, lane],
                seg,
                dest,
            )
        )
    own1 = pltpu.make_async_copy(own_g.at[:, cols(blk)], grads1.at[0, mine1], g1_recv.at[0, lane])
    own1.start()

    l_qacts.wait()
    rot_q[...] = jnp.dot(qacts[...], b_in[...], preferred_element_type=F32).astype(B16)
    l_eig.wait()
    inv[...] = 1.0 / (eig[...].astype(F32) + damping)
    l_bout.wait()

    @pl.when(jnp.logical_and(seg > 0, seg < segs - 1))
    def _():
        for q in range(queries):
            e_copy(q).wait_recv()
            advance(q)
            e_copy(q).start()

    def arrived(buf, sem, i, side, size):
        ref = buf.at[i, pl.ds(pl.multiple_of(side * size, size), size)]
        remote(ref, ref, sel_send.at[0], sem.at[i, side], seg, mate).wait_recv()

    def forward(buf, sem, fsem, rows_of, size):
        for off in range(1, chips):
            arrived(buf, sem, off, lane, size)
            ref = buf.at[off, rows_of]
            send(remote(ref, ref, fsem.at[off], sem.at[off, lane], seg, mate))

    forward(racts0, a0_recv, f0_send, mine0, tb)
    for i in range(chips):
        for side in range(2):
            arrived(grads0, g0_recv, i, side, tb)
        turned0[i] = jnp.dot(grads0[i], b_out[...], preferred_element_type=F32).astype(B16)
    forward(racts1, a1_recv, f1_send, mine1, half)
    for i in range(chips):
        arrived(racts0, a0_recv, i, mate_lane, tb)

    def core_of(q):
        return core_all[:, q * width : (q + 1) * width]

    def folded(x):
        x = sum(x[:, n * 128 : (n + 1) * 128] for n in range(width // 128))
        return jnp.sum(x, axis=0, keepdims=True)

    for q in range(queries):

        @pl.when(seg == 0)
        def _():
            e_copy(q).wait_recv()

        r = pl.ds(q * qt, qt)
        rot_e = jnp.dot(errs[r], b_out[...], preferred_element_type=F32).astype(B16)
        raw = lax.dot_general(
            rot_e, rot_q[r], (((0,), (0,)), ((), ())), preferred_element_type=F32
        )
        core_all[:, q * width : (q + 1) * width] = (raw * inv[...]).astype(B16)
        for i in range(chips):
            h = jnp.dot(turned0[i], core_of(q), preferred_element_type=F32)
            prod = h * racts0[i].astype(F32)
            for side in range(2):
                part[i, side, q : q + 1, :] = folded(prod[side * tb : (side + 1) * tb])

    for i in range(chips):
        for side in range(2):
            arrived(grads1, g1_recv, i, side, half)
        arrived(racts1, a1_recv, i, mate_lane, half)
    late = jnp.dot(
        grads1[...].reshape(chips * tb, width), b_out[...], preferred_element_type=F32
    ).astype(B16)
    for q in range(queries):
        h = jnp.dot(late, core_of(q), preferred_element_type=F32)
        prod = h * racts1[...].reshape(chips * tb, width).astype(F32)
        for i in range(chips):
            shared = folded(prod[i * tb : (i + 1) * tb])
            for side in range(2):
                part[i, side, queries + q : queries + q + 1, :] = shared

    values = 2 * queries
    tile = (chips, 2, values, 128)
    diag = lax.broadcasted_iota(jnp.int32, tile, 2) == lax.broadcasted_iota(jnp.int32, tile, 3)
    sums = jnp.sum(part[...], axis=3, keepdims=True)
    packed[...] = jnp.sum(jnp.where(diag, sums, 0.0), axis=2, keepdims=True)

    pl.semaphore_wait(ready, segs - 1)
    for seg_off in range(segs - 1, -1, -1):
        seg_to = lax.rem(seg + seg_off, segs)
        for off in range(chips):
            chip_to = lax.rem(chip + chips - off, chips)
            for turn in range(2):
                if seg_off == 0 and off == 0 and turn == 0:
                    continue
                side = lane if turn == 0 else mate_lane
                send(
                    remote(
                        packed.at[off, side],
                        gathered.at[seg, blk],
                        p_send.at[seg_off, off, turn],
                        p_recv.at[seg, blk],
                        seg_to,
                        chip_to * 2 + side,
                    )
                )
    gathered[seg, blk] = packed[0, lane]
    for seg_off in range(segs):
        for off in range(blks):
            if seg_off == 0 and off == 0:
                continue
            a, b = lax.rem(seg + seg_off, segs), lax.rem(blk + off, blks)
            ref = gathered.at[a, b]
            remote(ref, ref, sel_send.at[0], p_recv.at[a, b], seg, mate).wait_recv()
    total = jnp.sum(gathered[...].reshape(segs * blks, 128), axis=0, keepdims=True)
    tile = (values, 128)
    diag = lax.broadcasted_iota(jnp.int32, tile, 0) == lax.broadcasted_iota(jnp.int32, tile, 1)
    total = jnp.sum(jnp.where(diag, jnp.broadcast_to(total, tile), 0.0), axis=1, keepdims=True)
    out[:, 0:1] = total[0:queries]
    out[:, 1:2] = total[queries:values] * jnp.where(full, 1.0, 0.0)

    for copy in sends:
        copy.wait_send()

    @pl.when(seg > 0)
    def _():
        for q in range(queries):
            e_copy(q).wait_send()


def body(
    train_acts,
    train_grads,
    counts,
    basis_in,
    basis_out,
    eigenvalues,
    back_weight,
    derivative,
    query_acts,
    query_top,
):
    segs = lax.axis_size("seg")
    blks = lax.axis_size("blk")
    chips = blks // 2
    queries, qt, width = query_top.shape
    rows = train_acts.shape[1]
    tb = rows // SLOTS
    half = tb // 2
    wide = train_grads.shape[2]
    any_spec = pl.BlockSpec(memory_space=pltpu.HBM)
    vm = pltpu.VMEM
    dma = pltpu.SemaphoreType.DMA
    return pl.pallas_call(
        functools.partial(kernel, segs, blks, queries),
        out_shape=jax.ShapeDtypeStruct((queries, SLOTS), F32),
        in_specs=[pl.BlockSpec(memory_space=pltpu.SMEM)] + [any_spec] * 9,
        out_specs=pl.BlockSpec(memory_space=pltpu.VMEM),
        scratch_shapes=[
            vm((rows, width), B16),
            vm((half, wide), B16),
            vm((half, wide), B16),
            vm((half, width), B16),
            vm((width, width), B16),
            vm((width, width), B16),
            vm((width, width), B16),
            vm((width, width), B16),
            vm((queries * qt, width), B16),
            vm((queries * qt, width), B16),
            vm((queries * qt, width), B16),
            vm((queries * qt, width), B16),
            vm((width, width), F32),
            vm((queries * qt, width), B16),
            vm((width, queries * width), B16),
            vm((chips, 2 * tb, width), B16),
            vm((chips, 2 * half, width), B16),
            vm((chips, 2 * tb, width), B16),
            vm((chips, 2 * half, width), B16),
            vm((chips, 2 * tb, width), B16),
            vm((chips, 2, 2 * queries, 128), F32),
            vm((chips, 2, 1, 128), F32),
            vm((segs, blks, 1, 128), F32),
            dma((9,)),
            dma((2,)),
            dma((2,)),
            dma((chips, 2)),
            dma((chips, 2)),
            dma((chips, 2)),
            dma((chips, 2)),
            dma((chips,)),
            dma((chips, 2)),
            dma((chips,)),
            dma((chips, 2)),
            dma((chips,)),
            dma((chips,)),
            dma((queries,)),
            dma((queries,)),
            dma((segs, chips, 2)),
            dma((segs, blks)),
            pltpu.SemaphoreType.REGULAR,
        ],
        compiler_params=pltpu.CompilerParams(
            collective_id=0, has_side_effects=True, vmem_limit_bytes=67_043_328
        ),
    )(
        counts,
        train_acts[0],
        train_grads[0],
        basis_in[0, 0],
        basis_out[0, 0],
        eigenvalues[0, 0],
        back_weight[0, 0],
        derivative[0].reshape(queries * qt, width),
        query_acts[0].reshape(queries * qt, width),
        query_top.reshape(queries * qt, width),
    )


def solution(mesh):
    in_specs = (
        P("seg", "blk", None),
        P("seg", "blk", None),
        P(),
        P("seg", None, None, None),
        P("seg", "blk", None, None),
        P("seg", "blk", None, None),
        P("seg", "blk", None, None),
        P("seg", None, None, "blk"),
        P("seg", None, None, None),
        P(None, None, "blk"),
    )
    out_specs = P(None, "blk")
    return jax.shard_map(body, mesh=mesh, in_specs=in_specs, out_specs=out_specs, check_vma=False)
```
